32 devices in a mesh: ctx: 8 (over z, y), fsdp: 4 (over x, core).
Axes of the slice: x: 2, y: 2, z: 4, core: 2. Of those that a mesh axis runs over, the one named last changes fastest.
Arguments:
- tokens: bfloat16 [8, 1024, 960], P('fsdp', 'ctx'), may hold values from -6 to 6
- out_grad: bfloat16 [8, 1024, 960], P('fsdp', 'ctx'), may hold values from -6 to 6
- positions: int32 [8, 1024], P('fsdp', 'ctx'), may hold values from 0 to 3069, as said below
- query_weight: bfloat16 [960, 960], P('fsdp'), may hold values from -0.19364917 to 0.19364917
- key_weight: bfloat16 [960, 320], P('fsdp'), may hold values from -0.19364917 to 0.19364917
- value_weight: bfloat16 [960, 320], P('fsdp'), may hold values from -0.19364917 to 0.19364917
- output_weight: bfloat16 [960, 960], P('fsdp'), may hold values from -6 to 6
- gate_weight: bfloat16 [960, 2560], P('fsdp'), may hold values from -0.1875 to 0.1875
- up_weight: bfloat16 [960, 2560], P('fsdp'), may hold values from -0.1875 to 0.1875
- down_weight: bfloat16 [2560, 960], P('fsdp'), may hold values from -0.125 to 0.125
- first_gain: bfloat16 [960], P('fsdp'), may hold values from 0.5 to 1.5
- second_gain: bfloat16 [960], P('fsdp'), may hold values from 0.5 to 1.5
- query_momentum: float32 [960, 960], P('fsdp', 'ctx'), may hold values from -543.058 to 543.058
- key_momentum: float32 [960, 320], P('fsdp', 'ctx'), may hold values from -543.058 to 543.058
- value_momentum: float32 [960, 320], P('fsdp', 'ctx'), may hold values from -814.58701 to 814.58701
- output_momentum: float32 [960, 960], P('fsdp', 'ctx'), may hold values from -90.50967 to 90.50967
- gate_momentum: float32 [960, 2560], P('fsdp', 'ctx'), may hold values from -271.529 to 271.529
- up_momentum: float32 [960, 2560], P('fsdp', 'ctx'), may hold values from -271.529 to 271.529
- down_momentum: float32 [2560, 960], P('fsdp', 'ctx'), may hold values from -325.8348 to 325.8348
- first_momentum: float32 [960], P('fsdp'), may hold values from -160 to 160
- second_momentum: float32 [960], P('fsdp'), may hold values from -160 to 160
Outputs:
- layer_output: bfloat16 [8, 1024, 960], P('fsdp', 'ctx')
- input_grad: bfloat16 [8, 1024, 960], P('fsdp', 'ctx')
- query_grad: float32 [960, 960], P('fsdp', 'ctx')
- key_grad: float32 [960, 320], P('fsdp', 'ctx')
- value_grad: float32 [960, 320], P('fsdp', 'ctx')
- output_grad: float32 [960, 960], P('fsdp', 'ctx')
- gate_grad: float32 [960, 2560], P('fsdp', 'ctx')
- up_grad: float32 [960, 2560], P('fsdp', 'ctx')
- down_grad: float32 [2560, 960], P('fsdp', 'ctx')
- first_grad: float32 [960], P('fsdp')
- second_grad: float32 [960], P('fsdp')
- query_updated: float32 [960, 960], P('fsdp', 'ctx')
- key_updated: float32 [960, 320], P('fsdp', 'ctx')
- value_updated: float32 [960, 320], P('fsdp', 'ctx')
- output_updated: float32 [960, 960], P('fsdp', 'ctx')
- gate_updated: float32 [960, 2560], P('fsdp', 'ctx')
- up_updated: float32 [960, 2560], P('fsdp', 'ctx')
- down_updated: float32 [2560, 960], P('fsdp', 'ctx')
- first_updated: float32 [960], P('fsdp')
- second_updated: float32 [960], P('fsdp')
- query_velocity: float32 [960, 960], P('fsdp', 'ctx')
- key_velocity: float32 [960, 320], P('fsdp', 'ctx')
- value_velocity: float32 [960, 320], P('fsdp', 'ctx')
- output_velocity: float32 [960, 960], P('fsdp', 'ctx')
- gate_velocity: float32 [960, 2560], P('fsdp', 'ctx')
- up_velocity: float32 [960, 2560], P('fsdp', 'ctx')
- down_velocity: float32 [2560, 960], P('fsdp', 'ctx')
- first_velocity: float32 [960], P('fsdp')
- second_velocity: float32 [960], P('fsdp')
The draws below stay inside these ranges and needn't reach their ends.
Inputs may be any that keep to these rules, and one draw needn't show every extreme that they name: Each sequence starts at position 0 and its positions rise by 1 to 3 from one token to the next; in one sequence they rise by exactly 3 at every token.
All inputs are finite; a program needn't handle non-finite values.
Results may differ from the reference program's by a relative error of at most 0.04.
Values may be sent and summed in bfloat16 or wider, within the bound.
No kernel may reach another device: no remote copies, remote signals or barrier semaphores. Data moves between devices by JAX's collectives and lax.ppermute only.
A program may use at most 192 MiB of HBM per device.

```python
import math
import jax
import jax.numpy as jnp
from jax import lax

D = 960
FF = 2560
QUERY_HEADS = 15
KEY_HEADS = 5
HEAD_WIDTH = 64
QW = 960
KW = 320
QUERY_PER_KEY = 3
NMAT = 7
NS_ITERS = 5
SEQUENCE_COUNT = 8
SEQUENCE_TOKENS = 1024
TOKENS = 8192


def drawn_weight(key, salt, width_all):
    draw_key = jax.random.fold_in(key, salt)
    return (jnp.clip(jax.random.normal(draw_key, (D, width_all)), -6.0, 6.0) / D ** 0.5).astype(jnp.float32)


def draw_query_weight(key, part):
    return drawn_weight(key, 41, QW).astype(jnp.bfloat16)


def draw_key_weight(key, part):
    return drawn_weight(key, 42, KW).astype(jnp.bfloat16)


def draw_value_weight(key, part):
    return drawn_weight(key, 43, KW).astype(jnp.bfloat16)


def draw_tokens(key, part):
    noise_key = jax.random.fold_in(jax.random.fold_in(key, 11), 0)
    return jnp.clip(jax.random.normal(noise_key, (SEQUENCE_COUNT, SEQUENCE_TOKENS, D)), -6.0, 6.0).astype(jnp.bfloat16)


def draw_positions(key, part):
    gaps = jax.random.randint(jax.random.fold_in(key, 21), (SEQUENCE_COUNT, SEQUENCE_TOKENS), 1, 4)
    steady = jax.random.randint(jax.random.fold_in(key, 22), (), 0, SEQUENCE_COUNT)
    gaps = jnp.where((jnp.arange(SEQUENCE_COUNT) == steady)[:, None], 3, gaps)
    return (jnp.cumsum(gaps, axis=1) - gaps[:, :1]).astype(jnp.int32)


def state_draw(key, salt, row_count, column_count, level):
    row_key, column_key, noise_key = jax.random.split(jax.random.fold_in(key, salt), 3)
    row_scale = jnp.exp(jax.random.uniform(row_key, (row_count, 1), minval=-1.15, maxval=1.15))
    column_scale = jnp.exp(jax.random.uniform(column_key, (1, column_count), minval=-1.15, maxval=1.15))
    noise = jnp.clip(jax.random.normal(noise_key, (row_count, column_count)), -4.0, 4.0)
    return (level * TOKENS ** 0.5 / 4.0 * row_scale * column_scale * noise).astype(jnp.float32)


def draw_query_momentum(key, part):
    return state_draw(key, 51, D, QW, 0.6)


def draw_key_momentum(key, part):
    return state_draw(key, 52, D, KW, 0.6)


def draw_value_momentum(key, part):
    return state_draw(key, 53, D, KW, 0.9)


def draw_output_momentum(key, part):
    return state_draw(key, 54, QW, D, 0.1)


def draw_gate_momentum(key, part):
    return state_draw(key, 55, D, FF, 0.3)


def draw_up_momentum(key, part):
    return state_draw(key, 56, D, FF, 0.3)


def draw_down_momentum(key, part):
    return state_draw(key, 57, FF, D, 0.36)


def block_levels(rng, extent, pieces, smallest, top_value):
    level = 1.0
    for axis_at, blocks in pieces:
        draws = jax.random.uniform(jax.random.fold_in(jax.random.fold_in(rng, 6), axis_at), (blocks,), jnp.float32, smallest / len(pieces), top_value / len(pieces))
        level = level * jnp.repeat(jnp.exp(draws), extent[axis_at] // blocks).reshape((-1,) + (1,) * (len(extent) - 1 - axis_at))
    return level


def scatter_about(key, dims, scale, reach, shards=(), held_as=jnp.bfloat16):
    values = jax.random.normal(key, dims, jnp.float32) * scale
    if len(shards) > 0:
        values = block_levels(key, dims, shards, -0.22, 0.18) * values
    return jnp.clip(values, min=-reach, max=reach).astype(held_as)


def setup_inputs(seed: int = 0) -> dict:
    key_of = jax.random.split(jax.random.key(seed), 22)
    return {
        "tokens": draw_tokens(jax.random.fold_in(key_of[21], 71), 0),
        "out_grad": scatter_about(key_of[1], (SEQUENCE_COUNT, SEQUENCE_TOKENS, D), 1.0, 6.0, ((0, 4), (1, 8))),
        "positions": draw_positions(jax.random.fold_in(key_of[21], 71), 0),
        "query_weight": draw_query_weight(jax.random.fold_in(key_of[21], 71), 0),
        "key_weight": draw_key_weight(jax.random.fold_in(key_of[21], 71), 0),
        "value_weight": draw_value_weight(jax.random.fold_in(key_of[21], 71), 0),
        "output_weight": scatter_about(key_of[6], (QW, D), 1 ** -0.5, 6.0, ((0, 4),)),
        "gate_weight": scatter_about(key_of[7], (D, FF), D ** -0.5, 0.1875, ((0, 4),)),
        "up_weight": scatter_about(key_of[8], (D, FF), D ** -0.5, 0.1875, ((0, 4),)),
        "down_weight": scatter_about(key_of[9], (FF, D), FF ** -0.5, 0.125, ((0, 4),)),
        "first_gain": jnp.clip(1.0 + 0.1 * jax.random.normal(key_of[10], (D,), jnp.float32), 0.5, 1.5).astype(jnp.bfloat16),
        "second_gain": jnp.clip(1.0 + 0.1 * jax.random.normal(key_of[11], (D,), jnp.float32), 0.5, 1.5).astype(jnp.bfloat16),
        "query_momentum": draw_query_momentum(jax.random.fold_in(key_of[21], 71), 0),
        "key_momentum": draw_key_momentum(jax.random.fold_in(key_of[21], 71), 0),
        "value_momentum": draw_value_momentum(jax.random.fold_in(key_of[21], 71), 0),
        "output_momentum": draw_output_momentum(jax.random.fold_in(key_of[21], 71), 0),
        "gate_momentum": draw_gate_momentum(jax.random.fold_in(key_of[21], 71), 0),
        "up_momentum": draw_up_momentum(jax.random.fold_in(key_of[21], 71), 0),
        "down_momentum": draw_down_momentum(jax.random.fold_in(key_of[21], 71), 0),
        "first_momentum": scatter_about(key_of[19], (D,), (0.3 * TOKENS ** 0.5), 160.0, ((0, 4),), jnp.float32),
        "second_momentum": scatter_about(key_of[20], (D,), (0.3 * TOKENS ** 0.5), 160.0, ((0, 4),), jnp.float32),
    }


@jax.custom_vjp
def lowered_weights(v):
    return lax.optimization_barrier(v.astype(jnp.bfloat16)).astype(jnp.float32)

@jax.custom_vjp
def lowered_gradient(v):
    return v

def low_keep(v):
    return (lowered_weights(v), None)

def low_pass(kept, grad):
    return (grad,)

def back_keep(v):
    return (v, None)

def back_low(kept, grad):
    return (lowered_weights(grad),)
lowered_weights.defvjp(low_keep, low_pass)
lowered_gradient.defvjp(back_keep, back_low)
epsilon = 1e-05
rope_base = 100000.0
decay_rate = 0.9
step_rate = 0.2
newton_a = 3.4445
newton_b = -4.775
newton_c = 2.0315
masked_score = -1e+30
exact_precision = lax.Precision.HIGHEST

def rope_tables(positions):
    half_size = HEAD_WIDTH // 2
    frequency = rope_base ** (-(jnp.arange(half_size, dtype=jnp.float32) * 2.0) / HEAD_WIDTH)
    angles = positions.astype(jnp.float32)[..., None] * frequency
    return (jnp.cos(angles), jnp.sin(angles))

def apply_rotary(values, cosine_lookup, sine_lookup):
    half_size = values.shape[-1] // 2
    front_half = values[..., :half_size]
    back_half = values[..., half_size:]
    cosine = cosine_lookup[..., None, :]
    sine_part = sine_lookup[..., None, :]
    return jnp.concatenate([front_half * cosine - back_half * sine_part, back_half * cosine + front_half * sine_part], axis=-1)

def normalize(values, gain_vector):
    return values * lax.rsqrt(lax.optimization_barrier(jnp.mean(values * values, axis=-1, keepdims=True)) + epsilon) * gain_vector

def orthogonalize(matrix):
    flipped = matrix.shape[0] > matrix.shape[1]
    iterate = matrix.T if flipped else matrix
    iterate = lowered_weights(iterate / (jnp.sqrt(jnp.sum(iterate * iterate)) + 1e-07))
    for newton_step in range(NS_ITERS):
        gram_matrix = lowered_weights(jnp.dot(iterate, iterate.T, precision=exact_precision))
        square = jnp.dot(gram_matrix, gram_matrix, precision=exact_precision)
        polynomial = lowered_weights(newton_b * gram_matrix + newton_c * square)
        iterate = lowered_weights(newton_a * iterate + jnp.dot(polynomial, iterate, precision=exact_precision))
    return iterate.T if flipped else iterate

def reference(tokens, out_grad, positions, query_weight, key_weight, value_weight, output_weight, gate_weight, up_weight, down_weight, first_gain, second_gain, query_momentum, key_momentum, value_momentum, output_momentum, gate_momentum, up_momentum, down_momentum, first_momentum, second_momentum):
    cosine_lookup, sine_lookup = rope_tables(positions)
    rows_per_block = min(512, SEQUENCE_TOKENS)
    key_index = jnp.arange(SEQUENCE_TOKENS, dtype=jnp.int32)

    def attend_sequence(operands):
        query_rows, key_matrix_rows, value_matrix_rows = operands
        grouped_queries = query_rows.reshape(SEQUENCE_TOKENS // rows_per_block, rows_per_block, KEY_HEADS, QUERY_PER_KEY, HEAD_WIDTH)
        starts = jnp.arange(SEQUENCE_TOKENS // rows_per_block, dtype=jnp.int32) * rows_per_block

        def one_block(block_inputs):
            query_block, offset = block_inputs
            scores = jnp.einsum('qkgd,tkd->kgqt', query_block, key_matrix_rows, precision=exact_precision) * 0.125
            query_index = offset + jnp.arange(rows_per_block, dtype=jnp.int32)
            allowed = key_index[None, :] <= query_index[:, None]
            scores = lowered_gradient(jnp.where(allowed, scores, masked_score))
            probabilities = jax.nn.softmax(scores, axis=-1)
            mixed = jnp.einsum('kgqt,tkd->qkgd', lowered_weights(probabilities), value_matrix_rows, precision=exact_precision)
            return mixed.reshape(rows_per_block, QW)
        return lax.map(jax.checkpoint(one_block), (grouped_queries, starts)).reshape(SEQUENCE_TOKENS, QW)

    def forward(input_rows, gathered_query, gathered_key, gathered_value, gathered_output, gathered_gate, gathered_up, gathered_down, gain_one, gain_two):
        first_normed = lowered_weights(normalize(input_rows, gain_one))
        query_linear = lowered_gradient(jnp.einsum('ykr,ri->yki', first_normed, gathered_query, precision=exact_precision))
        key_linear = lowered_gradient(jnp.einsum('ykr,ri->yki', first_normed, gathered_key, precision=exact_precision))
        value_matrix_rows = lowered_weights(lowered_gradient(jnp.einsum('ykr,ri->yki', first_normed, gathered_value, precision=exact_precision)))
        value_matrix_rows = value_matrix_rows.reshape(SEQUENCE_COUNT, SEQUENCE_TOKENS, KEY_HEADS, HEAD_WIDTH)
        query_rows = lowered_weights(apply_rotary(query_linear.reshape(SEQUENCE_COUNT, SEQUENCE_TOKENS, QUERY_HEADS, HEAD_WIDTH), cosine_lookup, sine_lookup))
        key_matrix_rows = lowered_weights(apply_rotary(key_linear.reshape(SEQUENCE_COUNT, SEQUENCE_TOKENS, KEY_HEADS, HEAD_WIDTH), cosine_lookup, sine_lookup))
        attention_output = lax.map(attend_sequence, (query_rows, key_matrix_rows, value_matrix_rows))
        attention_output = lowered_weights(lowered_gradient(attention_output))
        residual_stream = input_rows + lowered_gradient(jnp.einsum('wxo,om->wxm', attention_output, gathered_output, precision=exact_precision))
        second_normed = lowered_weights(normalize(residual_stream, gain_two))
        gate_activation = lowered_gradient(jnp.einsum('yvn,nz->yvz', second_normed, gathered_gate, precision=exact_precision))
        up_linear = lowered_gradient(jnp.einsum('yvn,nz->yvz', second_normed, gathered_up, precision=exact_precision))
        hidden_state = lowered_weights(jax.nn.silu(gate_activation) * up_linear)
        return residual_stream + lowered_gradient(jnp.einsum('kzb,bn->kzn', hidden_state, gathered_down, precision=exact_precision))
    matrices = (query_weight.astype(jnp.float32), key_weight.astype(jnp.float32), value_weight.astype(jnp.float32), output_weight.astype(jnp.float32), gate_weight.astype(jnp.float32), up_weight.astype(jnp.float32), down_weight.astype(jnp.float32))
    gain_one = first_gain.astype(jnp.float32)
    gain_two = second_gain.astype(jnp.float32)
    input_rows = tokens.astype(jnp.float32)
    output_f32, pullback = jax.vjp(forward, input_rows, matrices[0], matrices[1], matrices[2], matrices[3], matrices[4], matrices[5], matrices[6], gain_one, gain_two)
    grads = pullback(out_grad.astype(jnp.float32))
    layer_output = output_f32.astype(jnp.bfloat16)
    input_grad = grads[0].astype(jnp.bfloat16)
    momenta = (query_momentum, key_momentum, value_momentum, output_momentum, gate_momentum, up_momentum, down_momentum)
    fans = (D, D, D, 1, D, D, FF)
    velocities = []
    updated = []
    for number in range(NMAT):
        velocity = decay_rate * momenta[number] + grads[number + 1]
        row_count, column_count = velocity.shape
        ortho = orthogonalize(lowered_weights(velocity))
        step_size = step_rate * math.sqrt(max(row_count, column_count) / fans[number])
        velocities.append(velocity)
        updated.append(matrices[number] - step_size * ortho)
    gain_rate = step_rate / math.sqrt(TOKENS)
    first_velocity = decay_rate * first_momentum + grads[8]
    second_velocity = decay_rate * second_momentum + grads[9]
    first_updated = gain_one - gain_rate * first_velocity
    second_updated = gain_two - gain_rate * second_velocity
    query_grad, key_grad, value_grad, output_grad, gate_grad, up_grad, down_grad, first_grad, second_grad = grads[1:]
    query_updated, key_updated, value_updated, output_updated, gate_updated, up_updated, down_updated = updated
    query_velocity, key_velocity, value_velocity, output_velocity, gate_velocity, up_velocity, down_velocity = velocities
    return (layer_output, input_grad, query_grad, key_grad, value_grad, output_grad, gate_grad, up_grad, down_grad, first_grad, second_grad, query_updated, key_updated, value_updated, output_updated, gate_updated, up_updated, down_updated, first_updated, second_updated, query_velocity, key_velocity, value_velocity, output_velocity, gate_velocity, up_velocity, down_velocity, first_velocity, second_velocity)
```

```python
import functools
import math

import jax
import jax.numpy as jnp
from jax import lax
from jax.experimental import pallas as pl
from jax.experimental.pallas import tpu as pltpu
from jax.sharding import PartitionSpec as P

D = 960
FF = 2560
QUERY_HEADS = 15
KEY_HEADS = 5
HEAD_WIDTH = 64
QW = 960
KW = 320
GROUP = QUERY_HEADS // KEY_HEADS
NS_ITERS = 5

EPSILON = 1e-05
ROPE_BASE = 100000.0
DECAY = 0.9
STEP_RATE = 0.2
NEWTON_A = 3.4445
NEWTON_B = -4.775
NEWTON_C = 2.0315
MASKED = -1e30
F32 = jnp.float32
BF16 = jnp.bfloat16


def einsum(spec, *operands):
    return jnp.einsum(spec, *operands, preferred_element_type=F32)


def after(value, *earlier):
    return lax.optimization_barrier((value,) + earlier)[0]


def swap(value, axis, size, mask):
    return lax.ppermute(value, axis, [(i, i ^ mask) for i in range(size)])


def masks_of(size):
    masks = []
    mask = size // 2
    while mask:
        masks.append(mask)
        mask //= 2
    return masks


def gather_ordered(block, axis, size, index, masks):
    current = block
    for mask in masks:
        other = swap(current, axis, size, mask)
        high = (index & mask) != 0
        current = jnp.stack([jnp.where(high, other, current), jnp.where(high, current, other)])
    bits = len(masks)
    order = {mask: bits - 1 - position for position, mask in enumerate(masks)}
    dims = [order[mask] for mask in masks_of(size)] + list(range(bits, bits + block.ndim))
    first = current.reshape((2,) * bits + block.shape)
    return jnp.transpose(first, dims).reshape((size,) + block.shape)


def gather_relative(block, axis, size, masks):
    current = block[None]
    offsets = [0]
    for mask in masks:
        other = swap(current, axis, size, mask)
        current = jnp.concatenate([current, other], axis=0)
        offsets = offsets + [offset ^ mask for offset in offsets]
    return current, offsets


def reduce_relative(parts, axis, size, masks):
    current = parts
    for mask in reversed(masks):
        half = current.shape[0] // 2
        other = swap(current[half:], axis, size, mask)
        total = current[:half].astype(F32) + other.astype(F32)
        current = total if half == 1 else total.astype(BF16)
    return current[0]


def reduce_ordered(parts, axis, size, index, masks):
    left = masks_of(size)
    current = parts.reshape((2,) * len(left) + parts.shape[1:])
    for number, mask in enumerate(masks):
        where = left.index(mask)
        bit = jnp.where((index & mask) != 0, 1, 0)
        keep = lax.dynamic_index_in_dim(current, bit, where, keepdims=False)
        send = lax.dynamic_index_in_dim(current, 1 - bit, where, keepdims=False)
        left.remove(mask)
        total = keep.astype(F32) + swap(send, axis, size, mask).astype(F32)
        current = total if number == len(masks) - 1 else total.astype(BF16)
    return current


def rotate(values, cosine, sine, sign):
    heads = values.reshape(-1, 2, HEAD_WIDTH // 2, values.shape[-1])
    front, back = heads[:, 0], heads[:, 1]
    turned = jnp.stack(
        [front * cosine - sign * back * sine, back * cosine + sign * front * sine], axis=1
    )
    return turned.reshape(values.shape)


def norm_parts(rows):
    return lax.rsqrt(jnp.mean(rows * rows, axis=-1, keepdims=True) + EPSILON)


def norm_back(rows, inverse, gain, grad):
    scaled = grad * gain
    mean = jnp.mean(scaled * rows, axis=-1, keepdims=True)
    back = inverse * scaled - rows * (inverse * inverse * inverse) * mean
    gain_grad = jnp.sum(grad * rows * inverse, axis=0)
    return back, gain_grad


def contract(left, right, left_axis, right_axis):
    return lax.dot_general(
        left, right, (((left_axis,), (right_axis,)), ((), ())), preferred_element_type=F32
    )


def side_by_side(ref, head, width=HEAD_WIDTH):
    first = head * GROUP
    return jnp.concatenate(
        [ref[(first + g) * width : (first + g + 1) * width, :] for g in range(GROUP)], axis=1
    )


def lag_table(length):
    row = lax.broadcasted_iota(jnp.int32, (length, GROUP * length), 0)
    lane = lax.broadcasted_iota(jnp.int32, (length, GROUP * length), 1)
    return row - lax.rem(lane, length)


def attend_kernel(offsets_k, offsets_v, me_ref, q_ref, k_ref, v_ref, out_ref, lse_ref):
    me = me_ref[0]
    length = q_ref.shape[1]
    lag = lag_table(length)
    place = {offset: p for p, offset in enumerate(offsets_v)}
    for head in range(KEY_HEADS):
        at = slice(head * HEAD_WIDTH, (head + 1) * HEAD_WIDTH)
        queries = side_by_side(q_ref, head)
        scores = []
        for p, offset in enumerate(offsets_k):
            block = contract(k_ref[p, at, :], queries, 0, 0)
            limit = (me - (me ^ offset)) * length
            scores.append(jnp.where(lag <= limit, block, MASKED))
        top = functools.reduce(jnp.maximum, [jnp.max(s, axis=0, keepdims=True) for s in scores])
        mass = jnp.zeros_like(top)
        mixed = jnp.zeros((HEAD_WIDTH, GROUP * length), F32)
        for p, offset in enumerate(offsets_k):
            weights = jnp.exp(scores[p] - top)
            mass = mass + jnp.sum(weights, axis=0, keepdims=True)
            mixed = mixed + contract(v_ref[place[offset], at, :], weights.astype(BF16), 1, 0)
        mixed = (mixed / mass).astype(BF16)
        lse = top + jnp.log(mass)
        for g in range(GROUP):
            first = (head * GROUP + g) * HEAD_WIDTH
            out_ref[first : first + HEAD_WIDTH, :] = mixed[:, g * length : (g + 1) * length]
            lse_ref[pl.ds(head * GROUP + g, 1), :] = lse[:, g * length : (g + 1) * length]


def attend_back_kernel(
    offsets_k, offsets_v, me_ref, q_ref, do_ref, lse_ref, k_ref, v_ref, cos_ref, sin_ref,
    dq_ref, dk_ref, dv_ref,
):
    me = me_ref[0]
    length = q_ref.shape[1]
    lag = lag_table(length)
    place = {offset: p for p, offset in enumerate(offsets_v)}
    cosine, sine = cos_ref[...], sin_ref[...]
    half = HEAD_WIDTH // 2
    for head in range(KEY_HEADS):
        at = slice(head * HEAD_WIDTH, (head + 1) * HEAD_WIDTH)
        queries = side_by_side(q_ref, head)
        grads = side_by_side(do_ref, head)
        lse = side_by_side(lse_ref, head, 1)
        chances, slopes = [], []
        delta = jnp.zeros_like(lse)
        for p, offset in enumerate(offsets_k):
            block = contract(k_ref[p, at, :], queries, 0, 0)
            limit = (me - (me ^ offset)) * length
            chance = jnp.exp(jnp.where(lag <= limit, block, MASKED) - lse)
            slope = contract(v_ref[place[offset], at, :], grads, 0, 0)
            delta = delta + jnp.sum(chance * slope, axis=0, keepdims=True)
            chances.append(chance)
            slopes.append(slope)
        back = jnp.zeros((HEAD_WIDTH, GROUP * length), F32)
        for p, offset in enumerate(offsets_k):
            low = (chances[p] * (slopes[p] - delta)).astype(BF16)
            back = back + contract(k_ref[p, at, :], low, 1, 0)
            dk_ref[p, at, :] = contract(queries, low, 1, 1).astype(BF16)
            dv_ref[place[offset], at, :] = contract(grads, chances[p].astype(BF16), 1, 1).astype(BF16)
        back = back * 0.125
        for g in range(GROUP):
            first = (head * GROUP + g) * HEAD_WIDTH
            part = back[:, g * length : (g + 1) * length]
            front, rear = part[:half], part[half:]
            dq_ref[first : first + half, :] = (front * cosine + rear * sine).astype(BF16)
            dq_ref[first + half : first + HEAD_WIDTH, :] = (rear * cosine - front * sine).astype(BF16)


def columns_spec(rows, length):
    return pl.BlockSpec((rows, length), lambda s: (0, s))


def blocks_spec(count, rows, length):
    return pl.BlockSpec((count, rows, length), lambda s: (0, 0, s))


def smem_spec():
    return pl.BlockSpec(memory_space=pltpu.SMEM)


def attend(me, queries, keys, values, offsets_k, offsets_v, sequences):
    tokens = queries.shape[1]
    length = tokens // sequences
    count = keys.shape[0]
    return pl.pallas_call(
        functools.partial(attend_kernel, offsets_k, offsets_v),
        grid=(sequences,),
        in_specs=[
            smem_spec(),
            columns_spec(QW, length),
            blocks_spec(count, KW, length),
            blocks_spec(count, KW, length),
        ],
        out_specs=[columns_spec(QW, length), columns_spec(16, length)],
        out_shape=[
            jax.ShapeDtypeStruct((QW, tokens), BF16),
            jax.ShapeDtypeStruct((16, tokens), F32),
        ],
        compiler_params=pltpu.CompilerParams(vmem_limit_bytes=40 << 20),
        cost_estimate=pl.CostEstimate(
            flops=4 * QW * tokens * count * length,
            bytes_accessed=2 * (2 * QW * tokens + 2 * count * KW * tokens),
            transcendentals=QUERY_HEADS * tokens * count * length,
        ),
        name="attend",
    )(me, queries, keys, values)


def attend_back(me, queries, grads, lse, keys, values, cosine, sine, offsets_k, offsets_v, sequences):
    tokens = queries.shape[1]
    length = tokens // sequences
    count = keys.shape[0]
    half = HEAD_WIDTH // 2
    return pl.pallas_call(
        functools.partial(attend_back_kernel, offsets_k, offsets_v),
        grid=(sequences,),
        in_specs=[
            smem_spec(),
            columns_spec(QW, length),
            columns_spec(QW, length),
            columns_spec(16, length),
            blocks_spec(count, KW, length),
            blocks_spec(count, KW, length),
            columns_spec(half, length),
            columns_spec(half, length),
        ],
        out_specs=[
            columns_spec(QW, length),
            blocks_spec(count, KW, length),
            blocks_spec(count, KW, length),
        ],
        out_shape=[
            jax.ShapeDtypeStruct((QW, tokens), BF16),
            jax.ShapeDtypeStruct((count, KW, tokens), BF16),
            jax.ShapeDtypeStruct((count, KW, tokens), BF16),
        ],
        compiler_params=pltpu.CompilerParams(vmem_limit_bytes=40 << 20),
        cost_estimate=pl.CostEstimate(
            flops=10 * QW * tokens * count * length,
            bytes_accessed=2 * (3 * QW * tokens + 4 * count * KW * tokens),
            transcendentals=QUERY_HEADS * tokens * count * length,
        ),
        name="attend_back",
    )(me, queries, grads, lse, keys, values, cosine, sine)


def orthogonalize(iterate):
    widened = iterate.astype(F32)
    iterate = (widened / (jnp.sqrt(jnp.sum(widened * widened)) + 1e-07)).astype(BF16)
    for _ in range(NS_ITERS):
        gram = einsum("rc,sc->rs", iterate, iterate).astype(BF16)
        square = einsum("rs,st->rt", gram, gram)
        polynomial = (NEWTON_B * gram.astype(F32) + NEWTON_C * square).astype(BF16)
        iterate = (NEWTON_A * iterate.astype(F32) + einsum("rs,sc->rc", polynomial, iterate)).astype(
            BF16
        )
    return iterate


def local(
    tokens, out_grad, positions,
    query_weight, key_weight, value_weight, output_weight, gate_weight, up_weight, down_weight,
    first_gain, second_gain,
    query_momentum, key_momentum, value_momentum, output_momentum, gate_momentum, up_momentum,
    down_momentum, first_momentum, second_momentum,
):
    C = lax.axis_size("ctx")
    F = lax.axis_size("fsdp")
    kc = lax.axis_index("ctx")
    fi = lax.axis_index("fsdp")
    S, L, _ = tokens.shape
    T = S * L
    ratio = C // F
    fmasks = masks_of(F)
    cmasks = masks_of(C)
    order_k = cmasks
    order_v = cmasks[-1:] + cmasks[:-1]
    R = D // F
    CD = D // C
    CK = KW // C
    CF = FF // C
    FS = FF // F

    tok = tokens.reshape(T, D).astype(F32)
    og = out_grad.reshape(T, D)
    pos = positions.reshape(T)

    gains = jnp.zeros((16, 2 * KW), BF16)
    gains = gains.at[0, :R].set(first_gain).at[1, :R].set(second_gain)
    kv_own = jnp.concatenate([jnp.concatenate([key_weight, value_weight], axis=1), gains], axis=0)
    kv_all = gather_ordered(kv_own, "fsdp", F, fi, fmasks)
    kv_full = kv_all[:, :R].reshape(D, 2 * KW)
    gain_one = kv_all[:, R, :R].reshape(D).astype(F32)
    gain_two = kv_all[:, R + 1, :R].reshape(D).astype(F32)
    q_full = gather_ordered(after(query_weight, kv_all), "fsdp", F, fi, fmasks).reshape(D, QW)

    half = HEAD_WIDTH // 2
    frequency = ROPE_BASE ** (-(jnp.arange(half, dtype=F32) * 2.0) / HEAD_WIDTH)
    angles = frequency[:, None] * pos.astype(F32)[None, :]
    cosine, sine = jnp.cos(angles), jnp.sin(angles)

    inverse_one = norm_parts(tok)
    x1 = (tok * inverse_one * gain_one).astype(BF16)
    kv_lin = einsum("td,dn->nt", x1, kv_full)
    keys_own = rotate(kv_lin[:KW], cosine, sine, 1.0).astype(BF16)
    values_own = kv_lin[KW:].astype(BF16)
    keys, offsets_k = gather_relative(keys_own, "ctx", C, order_k)
    values, offsets_v = gather_relative(values_own, "ctx", C, order_v)

    og_all, _ = gather_relative(after(og, q_full), "fsdp", F, fmasks)
    o_full = gather_ordered(after(output_weight, og_all), "fsdp", F, fi, fmasks).reshape(QW, D)

    def own_columns(weight, earlier):
        current = weight.reshape((R,) + (2,) * len(fmasks) + (FS,))
        current = after(current, earlier)
        for step, mask in enumerate(fmasks):
            bit = jnp.where((fi & mask) != 0, 1, 0)
            axis = 1 if step == 0 else 1 + step
            keep = lax.dynamic_index_in_dim(current, bit, axis, keepdims=False)
            send = lax.dynamic_index_in_dim(current, 1 - bit, axis, keepdims=False)
            other = swap(send, "fsdp", F, mask)
            high = (fi & mask) != 0
            current = jnp.stack([jnp.where(high, other, keep), jnp.where(high, keep, other)])
            current = jnp.moveaxis(current, 0, step)
        return current.reshape(D, FS)

    gate_cols = own_columns(gate_weight, o_full)
    up_cols = own_columns(up_weight, gate_cols)

    q_lin = einsum("td,dq->qt", x1, q_full)
    queries = (rotate(q_lin, cosine, sine, 1.0).astype(BF16) * 0.125).astype(BF16)
    me = kc.reshape(1).astype(jnp.int32)
    attended, lse = attend(me, queries, keys, values, offsets_k, offsets_v, S)
    residual = tok + einsum("qt,qd->td", attended, o_full)
    inverse_two = norm_parts(residual)
    x2 = (residual * inverse_two * gain_two).astype(BF16)

    x2_all, _ = gather_relative(x2, "fsdp", F, fmasks)
    x2_all = x2_all.reshape(F * T, D)
    og_all = og_all.reshape(F * T, D)
    gate = einsum("td,df->tf", x2_all, gate_cols)
    up = einsum("td,df->tf", x2_all, up_cols)
    sigma = jax.nn.sigmoid(gate)
    silu = gate * sigma
    hidden = (silu * up).astype(BF16)
    grad_hidden = einsum("td,fd->tf", og_all, down_weight)
    grad_gate = (grad_hidden * up * sigma * (1.0 + gate * (1.0 - sigma))).astype(BF16)
    grad_up = (grad_hidden * silu).astype(BF16)
    gn_parts = (
        einsum("tf,df->td", grad_gate, gate_cols) + einsum("tf,df->td", grad_up, up_cols)
    ).astype(BF16)
    grad_normed_two = reduce_relative(gn_parts.reshape(F, T, D), "fsdp", F, fmasks)
    down_parts = einsum("tf,fd->td", hidden, down_weight).astype(BF16)
    down_sum = reduce_relative(
        after(down_parts, grad_normed_two).reshape(F, T, D), "fsdp", F, fmasks
    )
    layer_output = (residual + down_sum).astype(BF16)

    mlp_parts = jnp.concatenate(
        [
            einsum("td,tf->df", x2_all, grad_gate).astype(BF16),
            einsum("td,tf->df", x2_all, grad_up).astype(BF16),
            einsum("td,tf->df", og_all, hidden).astype(BF16),
        ],
        axis=1,
    ).reshape(C, CD, 3 * FS)

    residual_part, second_part = norm_back(residual, inverse_two, gain_two, grad_normed_two)
    grad_residual = og.astype(F32) + residual_part
    grad_branch = grad_residual.astype(BF16)
    grad_attended = einsum("td,qd->qt", grad_branch, o_full).astype(BF16)
    grad_query, dk_parts, dv_parts = attend_back(
        me, queries, grad_attended, lse, keys, values, cosine, sine, offsets_k, offsets_v, S
    )
    key_rot = reduce_relative(dk_parts, "ctx", C, order_k)
    value_back = reduce_relative(dv_parts, "ctx", C, order_v)
    grad_key = rotate(key_rot, cosine, sine, -1.0).astype(BF16)
    grad_value = value_back.astype(BF16)

    def over_fsdp(parts):
        return reduce_ordered(parts.reshape(F, R, -1), "fsdp", F, fi, fmasks[::-1])

    def over_ctx(parts):
        return reduce_ordered(parts.astype(BF16), "ctx", C, kc, cmasks[::-1])

    mlp_sum = over_ctx(mlp_parts)
    down_grad = mlp_sum[:, 2 * FS :].T
    wide = mlp_sum[:, : 2 * FS].astype(BF16).reshape(CD, 2, ratio, CF)

    def holder(f, k, piece):
        return (ratio * f + piece) * F + k // ratio

    received = []
    for shift in range(ratio):
        piece = (kc + shift) % ratio
        pairs = []
        for f in range(F):
            for k in range(C):
                pairs.append((k * F + f, holder(f, k, (k + shift) % ratio)))
        sent = lax.dynamic_index_in_dim(wide, piece, 2, keepdims=False)
        received.append(lax.ppermute(sent, ("ctx", "fsdp"), pairs))
    stacked = jnp.stack(received)
    rows = []
    for j in range(ratio):
        shift = (kc - j) % ratio
        rows.append(lax.dynamic_index_in_dim(stacked, shift, 0, keepdims=False))
    wide_rows = jnp.concatenate(rows, axis=0).astype(F32)
    gate_grad, up_grad = wide_rows[:, 0], wide_rows[:, 1]

    output_parts = einsum("qt,td->qd", attended, grad_branch).astype(BF16)
    output_rows = over_fsdp(output_parts)
    output_grad = over_ctx(output_rows.T.reshape(C, CD, R)).T

    grads_all = jnp.concatenate([grad_query, grad_key, grad_value], axis=0)
    weights_all = jnp.concatenate([q_full, kv_full], axis=1)
    grad_normed_one = einsum("qt,dq->td", grads_all, weights_all)
    inputs_part, first_part = norm_back(tok, inverse_one, gain_one, grad_normed_one)
    input_grad = (grad_residual + inputs_part).astype(BF16)
    gain_columns = jnp.stack([first_part, second_part] + [jnp.zeros_like(first_part)] * 6, axis=1)
    qkv_parts = jnp.concatenate(
        [einsum("td,qt->dq", x1, grads_all).astype(BF16), gain_columns.astype(BF16)], axis=1
    )
    qkv_rows = over_fsdp(qkv_parts).T
    gain_block = jnp.broadcast_to(qkv_rows[None, QW + 2 * KW :], (C, 8, R))
    qkv_chunks = jnp.concatenate(
        [
            qkv_rows[:QW].reshape(C, CD, R),
            qkv_rows[QW : QW + KW].reshape(C, CK, R),
            qkv_rows[QW + KW : QW + 2 * KW].reshape(C, CK, R),
            gain_block,
        ],
        axis=1,
    )
    qkv_sum = over_ctx(qkv_chunks)
    query_grad = qkv_sum[:CD].T
    key_grad = qkv_sum[CD : CD + CK].T
    value_grad = qkv_sum[CD + CK : CD + 2 * CK].T
    first_grad = qkv_sum[CD + 2 * CK]
    second_grad = qkv_sum[CD + 2 * CK + 1]

    momenta = (
        query_momentum, key_momentum, value_momentum, output_momentum, gate_momentum, up_momentum,
        down_momentum,
    )
    grads = (query_grad, key_grad, value_grad, output_grad, gate_grad, up_grad, down_grad)
    velocities = [DECAY * momentum + grad for momentum, grad in zip(momenta, grads)]
    low = [velocity.astype(BF16) for velocity in velocities]

    def fold_down(block):
        turned = block.T
        return jnp.concatenate([turned[:, p * CF : (p + 1) * CF] for p in range(ratio)], axis=0)

    def unfold_down(block):
        return jnp.concatenate([block[p * CD : (p + 1) * CD] for p in range(ratio)], axis=1).T

    groups = jnp.stack(
        [low[4], fold_down(low[6]), low[5], jnp.concatenate([low[0], low[3], low[1], low[2]], axis=1)]
    )
    current = groups.reshape(2, 2, 1, R, CF)
    for step, mask in enumerate(fmasks):
        if step < 2:
            bit = jnp.where((fi & mask) != 0, 1, 0)
            keep = lax.dynamic_index_in_dim(current, bit, 0, keepdims=False)
            send = lax.dynamic_index_in_dim(current, 1 - bit, 0, keepdims=False)
        else:
            keep = send = current
        other = swap(send, "fsdp", F, mask)
        current = jnp.concatenate([keep, other], axis=-3)
    block = current
    owner_f = [g * (F // 4) for g in range(4)]
    owner_k = [2, 5, 2, 5] if C == 8 else [(5 * g + 2) % C for g in range(4)]
    gathered = [block]
    for r in range(1, C):
        pairs = [((owner_k[g] ^ r) * F + owner_f[g], owner_k[g] * F + owner_f[g]) for g in range(4)]
        gathered.append(lax.ppermute(block, ("ctx", "fsdp"), pairs))

    def wide_work(parts):
        matrix = jnp.concatenate([part.reshape(D, CF) for part in parts], axis=1)
        ortho = orthogonalize(matrix)
        return tuple(ortho[:, i * CF : (i + 1) * CF].reshape(F, R, CF) for i in range(C))

    def tall_work(parts):
        bands = [part.reshape(F * ratio, CD, CF) for part in parts]
        matrix = jnp.concatenate(
            [jnp.concatenate([band[i] for i in range(F * ratio)], axis=1) for band in bands], axis=0
        )
        ortho = orthogonalize(matrix)
        return tuple(
            jnp.stack(
                [
                    ortho[k * CD : (k + 1) * CD, i * CF : (i + 1) * CF]
                    for i in range(F * ratio)
                ]
            ).reshape(F, R, CF)
            for k in range(C)
        )

    def mixed_work(parts):
        def pick(first, width):
            return jnp.concatenate(
                [part.reshape(D, CF)[:, first : first + width] for part in parts], axis=1
            )

        query = orthogonalize(pick(0, CD))
        output = orthogonalize(pick(CD, CD))
        key = orthogonalize(pick(2 * CD, CK).T).T
        value = orthogonalize(pick(2 * CD + CK, CK).T).T
        return tuple(
            jnp.concatenate(
                [
                    query[:, i * CD : (i + 1) * CD],
                    output[:, i * CD : (i + 1) * CD],
                    key[:, i * CK : (i + 1) * CK],
                    value[:, i * CK : (i + 1) * CK],
                ],
                axis=1,
            ).reshape(F, R, CF)
            for i in range(C)
        )

    def no_work(parts):
        return tuple(jnp.zeros_like(part) for part in parts)

    owner = jnp.zeros((), jnp.bool_)
    for g in range(4):
        owner = owner | ((fi == owner_f[g]) & (kc == owner_k[g]))
    kind = jnp.where(fi == owner_f[3], 3, jnp.where(fi == owner_f[1], 2, 1))
    branch = jnp.where(owner, kind, 0)
    replies = lax.switch(branch, [no_work, wide_work, tall_work, mixed_work], tuple(gathered))
    reply = replies[0]
    for r in range(1, C):
        pairs = [(owner_k[g] * F + owner_f[g], (owner_k[g] ^ r) * F + owner_f[g]) for g in range(4)]
        reply = reply + lax.ppermute(replies[r], ("ctx", "fsdp"), pairs)
    current = reply
    for step in reversed(range(len(fmasks))):
        mask = fmasks[step]
        size = current.shape[-3] // 2
        keep = lax.slice_in_dim(current, 0, size, axis=current.ndim - 3)
        send = lax.slice_in_dim(current, size, 2 * size, axis=current.ndim - 3)
        other = swap(send, "fsdp", F, mask)
        high = (fi & mask) != 0
        if step < 2:
            current = jnp.stack([jnp.where(high, other, keep), jnp.where(high, keep, other)])
        else:
            current = jnp.where(high, other, keep)
    ortho_groups = current.reshape(4, R, CF)
    mixed = ortho_groups[3]
    orthos = [
        mixed[:, :CD],
        mixed[:, 2 * CD : 2 * CD + CK],
        mixed[:, 2 * CD + CK :],
        mixed[:, CD : 2 * CD],
        ortho_groups[0],
        ortho_groups[2],
        unfold_down(ortho_groups[1]),
    ]
    weights = (
        query_weight, key_weight, value_weight, output_weight, gate_weight, up_weight, down_weight,
    )
    fans = (D, D, D, 1, D, D, FF)
    shapes = ((D, QW), (D, KW), (D, KW), (QW, D), (D, FF), (D, FF), (FF, D))
    updated = []
    for number in range(7):
        total = shapes[number][1]
        width = total // C
        chosen = (
            lax.broadcasted_iota(jnp.int32, (total, width), 0)
            == lax.broadcasted_iota(jnp.int32, (total, width), 1) + kc * width
        ).astype(BF16)
        step_size = STEP_RATE * math.sqrt(max(shapes[number]) / fans[number])
        own = einsum("rc,cw->rw", weights[number], chosen)
        updated.append(own - step_size * orthos[number].astype(F32))
    gain_rate = STEP_RATE / math.sqrt(S * F * L * C)
    first_velocity = DECAY * first_momentum + first_grad
    second_velocity = DECAY * second_momentum + second_grad
    first_updated = first_gain.astype(F32) - gain_rate * first_velocity
    second_updated = second_gain.astype(F32) - gain_rate * second_velocity
    return (
        (layer_output.reshape(S, L, D), input_grad.reshape(S, L, D))
        + grads
        + (first_grad, second_grad)
        + tuple(updated)
        + (first_updated, second_updated)
        + tuple(velocities)
        + (first_velocity, second_velocity)
    )


def solution(mesh):
    rows = P("fsdp", None)
    block = P("fsdp", "ctx")
    line = P("fsdp")
    stream = P("fsdp", "ctx", None)
    in_specs = (stream, stream, block) + (rows,) * 7 + (line,) * 2 + (block,) * 7 + (line,) * 2
    out_specs = (stream, stream) + ((block,) * 7 + (line,) * 2) * 3
    return jax.shard_map(local, mesh=mesh, in_specs=in_specs, out_specs=out_specs, check_vma=False)
```

```python
import functools
import math

import jax
import jax.numpy as jnp
from jax import lax
from jax.experimental import pallas as pl
from jax.experimental.pallas import tpu as pltpu
from jax.sharding import PartitionSpec as P

D = 960
FF = 2560
QUERY_HEADS = 15
KEY_HEADS = 5
HEAD_WIDTH = 64
QW = 960
KW = 320
GROUP = QUERY_HEADS // KEY_HEADS
NS_ITERS = 5

EPSILON = 1e-05
ROPE_BASE = 100000.0
DECAY = 0.9
STEP_RATE = 0.2
NEWTON_A = 3.4445
NEWTON_B = -4.775
NEWTON_C = 2.0315
MASKED = -1e30
F32 = jnp.float32
BF16 = jnp.bfloat16


def einsum(spec, *operands):
    return jnp.einsum(spec, *operands, preferred_element_type=F32)


def after(value, *earlier):
    return lax.optimization_barrier((value,) + earlier)[0]


def swap(value, axis, size, mask):
    return lax.ppermute(value, axis, [(i, i ^ mask) for i in range(size)])


def masks_of(size):
    masks = []
    mask = size // 2
    while mask:
        masks.append(mask)
        mask //= 2
    return masks


def gather_ordered(block, axis, size, index, masks):
    current = block
    for mask in masks:
        other = swap(current, axis, size, mask)
        high = (index & mask) != 0
        current = jnp.stack([jnp.where(high, other, current), jnp.where(high, current, other)])
    bits = len(masks)
    order = {mask: bits - 1 - position for position, mask in enumerate(masks)}
    dims = [order[mask] for mask in masks_of(size)] + list(range(bits, bits + block.ndim))
    first = current.reshape((2,) * bits + block.shape)
    return jnp.transpose(first, dims).reshape((size,) + block.shape)


def gather_relative(block, axis, size, masks):
    current = block[None]
    offsets = [0]
    for mask in masks:
        other = swap(current, axis, size, mask)
        current = jnp.concatenate([current, other], axis=0)
        offsets = offsets + [offset ^ mask for offset in offsets]
    return current, offsets


def reduce_relative(parts, axis, size, masks):
    current = parts
    for mask in reversed(masks):
        half = current.shape[0] // 2
        other = swap(current[half:], axis, size, mask)
        total = current[:half].astype(F32) + other.astype(F32)
        current = total if half == 1 else total.astype(BF16)
    return current[0]


def reduce_ordered(parts, axis, size, index, masks):
    left = masks_of(size)
    current = parts.reshape((2,) * len(left) + parts.shape[1:])
    for number, mask in enumerate(masks):
        where = left.index(mask)
        bit = jnp.where((index & mask) != 0, 1, 0)
        keep = lax.dynamic_index_in_dim(current, bit, where, keepdims=False)
        send = lax.dynamic_index_in_dim(current, 1 - bit, where, keepdims=False)
        left.remove(mask)
        total = keep.astype(F32) + swap(send, axis, size, mask).astype(F32)
        current = total if number == len(masks) - 1 else total.astype(BF16)
    return current


def rotate(values, cosine, sine, sign):
    heads = values.reshape(-1, 2, HEAD_WIDTH // 2, values.shape[-1])
    front, back = heads[:, 0], heads[:, 1]
    turned = jnp.stack(
        [front * cosine - sign * back * sine, back * cosine + sign * front * sine], axis=1
    )
    return turned.reshape(values.shape)


def norm_parts(rows):
    return lax.rsqrt(jnp.mean(rows * rows, axis=-1, keepdims=True) + EPSILON)


def norm_back(rows, inverse, gain, grad):
    scaled = grad * gain
    mean = jnp.mean(scaled * rows, axis=-1, keepdims=True)
    back = inverse * scaled - rows * (inverse * inverse * inverse) * mean
    gain_grad = jnp.sum(grad * rows * inverse, axis=0)
    return back, gain_grad


def contract(left, right, left_axis, right_axis):
    return lax.dot_general(
        left, right, (((left_axis,), (right_axis,)), ((), ())), preferred_element_type=F32
    )


def side_by_side(ref, head, width=HEAD_WIDTH):
    first = head * GROUP
    return jnp.concatenate(
        [ref[(first + g) * width : (first + g + 1) * width, :] for g in range(GROUP)], axis=1
    )


def lag_table(length):
    row = lax.broadcasted_iota(jnp.int32, (length, GROUP * length), 0)
    lane = lax.broadcasted_iota(jnp.int32, (length, GROUP * length), 1)
    return row - lax.rem(lane, length)


def attend_kernel(offsets_k, offsets_v, me_ref, q_ref, k_ref, v_ref, out_ref, lse_ref):
    me = me_ref[0]
    length = q_ref.shape[1]
    lag = lag_table(length)
    place = {offset: p for p, offset in enumerate(offsets_v)}
    for head in range(KEY_HEADS):
        at = slice(head * HEAD_WIDTH, (head + 1) * HEAD_WIDTH)
        queries = side_by_side(q_ref, head)
        scores = []
        for p, offset in enumerate(offsets_k):
            block = contract(k_ref[p, at, :], queries, 0, 0)
            limit = (me - (me ^ offset)) * length
            scores.append(jnp.where(lag <= limit, block, MASKED))
        top = functools.reduce(jnp.maximum, [jnp.max(s, axis=0, keepdims=True) for s in scores])
        mass = jnp.zeros_like(top)
        mixed = jnp.zeros((HEAD_WIDTH, GROUP * length), F32)
        for p, offset in enumerate(offsets_k):
            weights = jnp.exp(scores[p] - top)
            mass = mass + jnp.sum(weights, axis=0, keepdims=True)
            mixed = mixed + contract(v_ref[place[offset], at, :], weights.astype(BF16), 1, 0)
        mixed = (mixed / mass).astype(BF16)
        lse = top + jnp.log(mass)
        for g in range(GROUP):
            first = (head * GROUP + g) * HEAD_WIDTH
            out_ref[first : first + HEAD_WIDTH, :] = mixed[:, g * length : (g + 1) * length]
            lse_ref[pl.ds(head * GROUP + g, 1), :] = lse[:, g * length : (g + 1) * length]


def attend_back_kernel(
    offsets_k, offsets_v, me_ref, q_ref, do_ref, lse_ref, k_ref, v_ref, cos_ref, sin_ref,
    dq_ref, dk_ref, dv_ref,
):
    me = me_ref[0]
    length = q_ref.shape[1]
    lag = lag_table(length)
    place = {offset: p for p, offset in enumerate(offsets_v)}
    cosine, sine = cos_ref[...], sin_ref[...]
    half = HEAD_WIDTH // 2
    for head in range(KEY_HEADS):
        at = slice(head * HEAD_WIDTH, (head + 1) * HEAD_WIDTH)
        queries = side_by_side(q_ref, head)
        grads = side_by_side(do_ref, head)
        lse = side_by_side(lse_ref, head, 1)
        chances, slopes = [], []
        delta = jnp.zeros_like(lse)
        for p, offset in enumerate(offsets_k):
            block = contract(k_ref[p, at, :], queries, 0, 0)
            limit = (me - (me ^ offset)) * length
            chance = jnp.exp(jnp.where(lag <= limit, block, MASKED) - lse)
            slope = contract(v_ref[place[offset], at, :], grads, 0, 0)
            delta = delta + jnp.sum(chance * slope, axis=0, keepdims=True)
            chances.append(chance)
            slopes.append(slope)
        back = jnp.zeros((HEAD_WIDTH, GROUP * length), F32)
        for p, offset in enumerate(offsets_k):
            low = (chances[p] * (slopes[p] - delta)).astype(BF16)
            back = back + contract(k_ref[p, at, :], low, 1, 0)
            dk_ref[p, at, :] = contract(queries, low, 1, 1).astype(BF16)
            dv_ref[place[offset], at, :] = contract(grads, chances[p].astype(BF16), 1, 1).astype(BF16)
        back = back * 0.125
        for g in range(GROUP):
            first = (head * GROUP + g) * HEAD_WIDTH
            part = back[:, g * length : (g + 1) * length]
            front, rear = part[:half], part[half:]
            dq_ref[first : first + half, :] = (front * cosine + rear * sine).astype(BF16)
            dq_ref[first + half : first + HEAD_WIDTH, :] = (rear * cosine - front * sine).astype(BF16)


def columns_spec(rows, length):
    return pl.BlockSpec((rows, length), lambda s: (0, s))


def blocks_spec(count, rows, length):
    return pl.BlockSpec((count, rows, length), lambda s: (0, 0, s))


def smem_spec():
    return pl.BlockSpec(memory_space=pltpu.SMEM)


def attend(me, queries, keys, values, offsets_k, offsets_v, sequences):
    tokens = queries.shape[1]
    length = tokens // sequences
    count = keys.shape[0]
    return pl.pallas_call(
        functools.partial(attend_kernel, offsets_k, offsets_v),
        grid=(sequences,),
        in_specs=[
            smem_spec(),
            columns_spec(QW, length),
            blocks_spec(count, KW, length),
            blocks_spec(count, KW, length),
        ],
        out_specs=[columns_spec(QW, length), columns_spec(16, length)],
        out_shape=[
            jax.ShapeDtypeStruct((QW, tokens), BF16),
            jax.ShapeDtypeStruct((16, tokens), F32),
        ],
        compiler_params=pltpu.CompilerParams(vmem_limit_bytes=40 << 20),
        cost_estimate=pl.CostEstimate(
            flops=4 * QW * tokens * count * length,
            bytes_accessed=2 * (2 * QW * tokens + 2 * count * KW * tokens),
            transcendentals=QUERY_HEADS * tokens * count * length,
        ),
        name="attend",
    )(me, queries, keys, values)


def attend_back(me, queries, grads, lse, keys, values, cosine, sine, offsets_k, offsets_v, sequences):
    tokens = queries.shape[1]
    length = tokens // sequences
    count = keys.shape[0]
    half = HEAD_WIDTH // 2
    return pl.pallas_call(
        functools.partial(attend_back_kernel, offsets_k, offsets_v),
        grid=(sequences,),
        in_specs=[
            smem_spec(),
            columns_spec(QW, length),
            columns_spec(QW, length),
            columns_spec(16, length),
            blocks_spec(count, KW, length),
            blocks_spec(count, KW, length),
            columns_spec(half, length),
            columns_spec(half, length),
        ],
        out_specs=[
            columns_spec(QW, length),
            blocks_spec(count, KW, length),
            blocks_spec(count, KW, length),
        ],
        out_shape=[
            jax.ShapeDtypeStruct((QW, tokens), BF16),
            jax.ShapeDtypeStruct((count, KW, tokens), BF16),
            jax.ShapeDtypeStruct((count, KW, tokens), BF16),
        ],
        compiler_params=pltpu.CompilerParams(vmem_limit_bytes=40 << 20),
        cost_estimate=pl.CostEstimate(
            flops=10 * QW * tokens * count * length,
            bytes_accessed=2 * (3 * QW * tokens + 4 * count * KW * tokens),
            transcendentals=QUERY_HEADS * tokens * count * length,
        ),
        name="attend_back",
    )(me, queries, grads, lse, keys, values, cosine, sine)


def lanes_up(width):
    return -(-width // 128) * 128


def newton_schulz(x_ref, gram_ref, poly_ref, count, width, chunk):
    rows = [(i, min(256, count - i)) for i in range(0, count, 256)]

    def iteration(_, carry):
        for i, h in rows:
            block = contract(x_ref[i : i + h, :width], x_ref[i:count, :width], 1, 1).astype(BF16)
            gram_ref[i : i + h, i:count] = block
            if i + h < count:
                gram_ref[i + h : count, i : i + h] = block[:, h:].T
        for i, h in rows:
            line = gram_ref[i : i + h, :count]
            square = contract(line, gram_ref[:count, i:count], 1, 0)
            block = (NEWTON_B * line[:, i:].astype(F32) + NEWTON_C * square).astype(BF16)
            poly_ref[i : i + h, i:count] = block
            if i + h < count:
                poly_ref[i + h : count, i : i + h] = block[:, h:].T

        @pl.loop(0, width // chunk)
        def _(c):
            at = pl.ds(pl.multiple_of(c * chunk, chunk), chunk)
            old = x_ref[:count, at]
            new = NEWTON_A * old.astype(F32) + contract(poly_ref[:count, :count], old, 1, 0)
            x_ref[:count, at] = new.astype(BF16)

        return carry

    lax.fori_loop(0, NS_ITERS, iteration, 0)


def owner_kernel(F, C, role_ref, *refs):
    parts, outs = refs[:C], refs[C : 2 * C]
    wide_ref, x_ref, gram_ref, poly_ref = refs[2 * C :]
    R, CF = parts[0].shape[1:]
    ratio = C // F
    CD = D // C
    CK = KW // C
    RP = lanes_up(R)
    main = CF // 128 * 128
    rest = CF - main
    role = role_ref[0]

    def pieces(i):
        return ((0, main, i * main), (main, rest, C * main + i * rest))

    def scaled(count, width):
        whole = wide_ref[:count, :width]
        scale = 1.0 / (jnp.sqrt(jnp.sum(whole * whole)) + 1e-07)
        x_ref[:count, :width] = (whole * scale).astype(BF16)

    def widen(count, width):
        wide_ref[:count, :width] = x_ref[:count, :width].astype(F32)

    def wide_moves(move):
        for k in range(C):
            @pl.loop(0, F)
            def _(f):
                for source, width, target in pieces(k):
                    move(
                        (k, f, slice(None), slice(source, source + width)),
                        (pl.ds(pl.multiple_of(f * R, 8), R), slice(target, target + width)),
                    )

    def tall_moves(move):
        for k in range(C):
            for f in range(F):
                for p in range(ratio):
                    for source, width, target in pieces(f * ratio + p):
                        move(
                            (k, f, slice(p * CD, (p + 1) * CD), slice(source, source + width)),
                            (slice(k * CD, (k + 1) * CD), slice(target, target + width)),
                        )

    def take(source, target):
        wide_ref[target] = parts[source[0]][source[1:]].astype(F32)

    def give(source, target):
        outs[source[0]][source[1:]] = wide_ref[target].astype(BF16)

    @pl.when(role == 1)
    def _():
        wide_moves(take)

    @pl.when(role == 2)
    def _():
        tall_moves(take)

    @pl.when((role == 1) | (role == 2))
    def _():
        scaled(D, FF)
        newton_schulz(x_ref, gram_ref, poly_ref, D, FF, 512)
        widen(D, FF)

    @pl.when(role == 1)
    def _():
        wide_moves(give)

    @pl.when(role == 2)
    def _():
        tall_moves(give)

    @pl.when(role == 3)
    def _():
        span = F * RP
        third = CF - R

        def square_moves(move, first):
            for k in range(C):
                for f in range(F):
                    move(
                        (k, f, slice(first, first + CD), slice(0, R)),
                        (slice(k * CD, (k + 1) * CD), slice(f * RP, f * RP + R)),
                    )

        def narrow_moves(move, first):
            for k in range(C):
                for f in range(F):
                    for p in range(R // third):
                        at = p * 2 * CK + first
                        lane = f * RP + p * third
                        move(
                            (k, f, slice(at, at + CK), slice(R, CF)),
                            (slice(k * CK, (k + 1) * CK), slice(lane, lane + third)),
                        )

        for moves, count, step in ((square_moves, D, CD), (narrow_moves, KW, CK)):

            @pl.loop(0, 2)
            def _(turn):
                wide_ref[:count, :span] = jnp.zeros((count, span), F32)
                for side in range(2):

                    @pl.when(turn == side)
                    def _():
                        moves(take, side * step)

                scaled(count, span)
                newton_schulz(x_ref, gram_ref, poly_ref, count, span, min(span, 512))
                widen(count, span)
                for side in range(2):

                    @pl.when(turn == side)
                    def _():
                        moves(give, side * step)


def owner_step(role, parts, F, C):
    shape = jax.ShapeDtypeStruct(parts[0].shape, BF16)
    vmem = pl.BlockSpec(memory_space=pltpu.VMEM)
    return pl.pallas_call(
        functools.partial(owner_kernel, F, C),
        in_specs=[smem_spec()] + [vmem] * C,
        out_specs=[vmem] * C,
        out_shape=[shape] * C,
        scratch_shapes=[
            pltpu.VMEM((D, FF), F32),
            pltpu.VMEM((D, FF), BF16),
            pltpu.VMEM((D, D), BF16),
            pltpu.VMEM((D, D), BF16),
        ],
        compiler_params=pltpu.CompilerParams(vmem_limit_bytes=60 << 20),
        cost_estimate=pl.CostEstimate(flops=56 * 10**9, bytes_accessed=4 * D * FF, transcendentals=0),
        name="newton_schulz",
    )(role, *parts)


def local(
    tokens, out_grad, positions,
    query_weight, key_weight, value_weight, output_weight, gate_weight, up_weight, down_weight,
    first_gain, second_gain,
    query_momentum, key_momentum, value_momentum, output_momentum, gate_momentum, up_momentum,
    down_momentum, first_momentum, second_momentum,
):
    C = lax.axis_size("ctx")
    F = lax.axis_size("fsdp")
    kc = lax.axis_index("ctx")
    fi = lax.axis_index("fsdp")
    S, L, _ = tokens.shape
    T = S * L
    ratio = C // F
    fmasks = masks_of(F)
    cmasks = masks_of(C)
    order_k = cmasks
    order_v = cmasks[-1:] + cmasks[:-1]
    R = D // F
    CD = D // C
    CK = KW // C
    CF = FF // C
    FS = FF // F

    tok = tokens.reshape(T, D).astype(F32)
    og = out_grad.reshape(T, D)
    pos = positions.reshape(T)

    gains = jnp.zeros((16, 2 * KW), BF16)
    gains = gains.at[0, :R].set(first_gain).at[1, :R].set(second_gain)
    kv_own = jnp.concatenate([jnp.concatenate([key_weight, value_weight], axis=1), gains], axis=0)
    kv_all = gather_ordered(kv_own, "fsdp", F, fi, fmasks)
    kv_full = kv_all[:, :R].reshape(D, 2 * KW)
    gain_one = kv_all[:, R, :R].reshape(D).astype(F32)
    gain_two = kv_all[:, R + 1, :R].reshape(D).astype(F32)
    q_full = gather_ordered(after(query_weight, kv_all), "fsdp", F, fi, fmasks).reshape(D, QW)

    half = HEAD_WIDTH // 2
    frequency = ROPE_BASE ** (-(jnp.arange(half, dtype=F32) * 2.0) / HEAD_WIDTH)
    angles = frequency[:, None] * pos.astype(F32)[None, :]
    cosine, sine = jnp.cos(angles), jnp.sin(angles)

    inverse_one = norm_parts(tok)
    x1 = (tok * inverse_one * gain_one).astype(BF16)
    kv_lin = einsum("td,dn->nt", x1, kv_full)
    keys_own = rotate(kv_lin[:KW], cosine, sine, 1.0).astype(BF16)
    values_own = kv_lin[KW:].astype(BF16)
    keys, offsets_k = gather_relative(keys_own, "ctx", C, order_k)
    values, offsets_v = gather_relative(values_own, "ctx", C, order_v)

    og_all, _ = gather_relative(after(og, q_full), "fsdp", F, fmasks)
    o_full = gather_ordered(after(output_weight, og_all), "fsdp", F, fi, fmasks).reshape(QW, D)

    def own_columns(weight, earlier):
        current = weight.reshape((R,) + (2,) * len(fmasks) + (FS,))
        current = after(current, earlier)
        for step, mask in enumerate(fmasks):
            bit = jnp.where((fi & mask) != 0, 1, 0)
            axis = 1 if step == 0 else 1 + step
            keep = lax.dynamic_index_in_dim(current, bit, axis, keepdims=False)
            send = lax.dynamic_index_in_dim(current, 1 - bit, axis, keepdims=False)
            other = swap(send, "fsdp", F, mask)
            high = (fi & mask) != 0
            current = jnp.stack([jnp.where(high, other, keep), jnp.where(high, keep, other)])
            current = jnp.moveaxis(current, 0, step)
        return current.reshape(D, FS)

    gate_cols = own_columns(gate_weight, o_full)
    up_cols = own_columns(up_weight, gate_cols)

    q_lin = einsum("td,dq->qt", x1, q_full)
    queries = (rotate(q_lin, cosine, sine, 1.0).astype(BF16) * 0.125).astype(BF16)
    me = kc.reshape(1).astype(jnp.int32)
    attended, lse = attend(me, queries, keys, values, offsets_k, offsets_v, S)
    residual = tok + einsum("qt,qd->td", attended, o_full)
    inverse_two = norm_parts(residual)
    x2 = (residual * inverse_two * gain_two).astype(BF16)

    x2_all, _ = gather_relative(x2, "fsdp", F, fmasks)
    x2_all = x2_all.reshape(F * T, D)
    og_all = og_all.reshape(F * T, D)
    gate = einsum("td,df->tf", x2_all, gate_cols)
    up = einsum("td,df->tf", x2_all, up_cols)
    sigma = jax.nn.sigmoid(gate)
    silu = gate * sigma
    hidden = (silu * up).astype(BF16)
    grad_hidden = einsum("td,fd->tf", og_all, down_weight)
    grad_gate = (grad_hidden * up * sigma * (1.0 + gate * (1.0 - sigma))).astype(BF16)
    grad_up = (grad_hidden * silu).astype(BF16)
    gn_parts = (
        einsum("tf,df->td", grad_gate, gate_cols) + einsum("tf,df->td", grad_up, up_cols)
    ).astype(BF16)
    grad_normed_two = reduce_relative(gn_parts.reshape(F, T, D), "fsdp", F, fmasks)
    down_parts = einsum("tf,fd->td", hidden, down_weight).astype(BF16)
    down_sum = reduce_relative(
        after(down_parts, grad_normed_two).reshape(F, T, D), "fsdp", F, fmasks
    )
    layer_output = (residual + down_sum).astype(BF16)

    mlp_parts = jnp.concatenate(
        [
            einsum("td,tf->df", x2_all, grad_gate).astype(BF16),
            einsum("td,tf->df", x2_all, grad_up).astype(BF16),
            einsum("td,tf->df", og_all, hidden).astype(BF16),
        ],
        axis=1,
    ).reshape(C, CD, 3 * FS)

    residual_part, second_part = norm_back(residual, inverse_two, gain_two, grad_normed_two)
    grad_residual = og.astype(F32) + residual_part
    grad_branch = grad_residual.astype(BF16)
    grad_attended = einsum("td,qd->qt", grad_branch, o_full).astype(BF16)
    grad_query, dk_parts, dv_parts = attend_back(
        me, queries, grad_attended, lse, keys, values, cosine, sine, offsets_k, offsets_v, S
    )
    key_rot = reduce_relative(dk_parts, "ctx", C, order_k)
    value_back = reduce_relative(dv_parts, "ctx", C, order_v)
    grad_key = rotate(key_rot, cosine, sine, -1.0).astype(BF16)
    grad_value = value_back.astype(BF16)

    def over_fsdp(parts):
        return reduce_ordered(parts.reshape(F, R, -1), "fsdp", F, fi, fmasks[::-1])

    def over_ctx(parts):
        return reduce_ordered(parts.astype(BF16), "ctx", C, kc, cmasks[::-1])

    mlp_sum = over_ctx(mlp_parts)
    down_grad = mlp_sum[:, 2 * FS :].T
    wide = mlp_sum[:, : 2 * FS].astype(BF16).reshape(CD, 2, ratio, CF)

    def holder(f, k, piece):
        return (ratio * f + piece) * F + k // ratio

    received = []
    for shift in range(ratio):
        piece = (kc + shift) % ratio
        pairs = []
        for f in range(F):
            for k in range(C):
                pairs.append((k * F + f, holder(f, k, (k + shift) % ratio)))
        sent = lax.dynamic_index_in_dim(wide, piece, 2, keepdims=False)
        received.append(lax.ppermute(sent, ("ctx", "fsdp"), pairs))
    stacked = jnp.stack(received)
    rows = []
    for j in range(ratio):
        shift = (kc - j) % ratio
        rows.append(lax.dynamic_index_in_dim(stacked, shift, 0, keepdims=False))
    wide_rows = jnp.concatenate(rows, axis=0).astype(F32)
    gate_grad, up_grad = wide_rows[:, 0], wide_rows[:, 1]

    output_parts = einsum("qt,td->qd", attended, grad_branch).astype(BF16)
    output_rows = over_fsdp(output_parts)
    output_grad = over_ctx(output_rows.T.reshape(C, CD, R)).T

    grads_all = jnp.concatenate([grad_query, grad_key, grad_value], axis=0)
    weights_all = jnp.concatenate([q_full, kv_full], axis=1)
    grad_normed_one = einsum("qt,dq->td", grads_all, weights_all)
    inputs_part, first_part = norm_back(tok, inverse_one, gain_one, grad_normed_one)
    input_grad = (grad_residual + inputs_part).astype(BF16)
    gain_columns = jnp.stack([first_part, second_part] + [jnp.zeros_like(first_part)] * 6, axis=1)
    qkv_parts = jnp.concatenate(
        [einsum("td,qt->dq", x1, grads_all).astype(BF16), gain_columns.astype(BF16)], axis=1
    )
    qkv_rows = over_fsdp(qkv_parts).T
    gain_block = jnp.broadcast_to(qkv_rows[None, QW + 2 * KW :], (C, 8, R))
    qkv_chunks = jnp.concatenate(
        [
            qkv_rows[:QW].reshape(C, CD, R),
            qkv_rows[QW : QW + KW].reshape(C, CK, R),
            qkv_rows[QW + KW : QW + 2 * KW].reshape(C, CK, R),
            gain_block,
        ],
        axis=1,
    )
    qkv_sum = over_ctx(qkv_chunks)
    query_grad = qkv_sum[:CD].T
    key_grad = qkv_sum[CD : CD + CK].T
    value_grad = qkv_sum[CD + CK : CD + 2 * CK].T
    first_grad = qkv_sum[CD + 2 * CK]
    second_grad = qkv_sum[CD + 2 * CK + 1]

    momenta = (
        query_momentum, key_momentum, value_momentum, output_momentum, gate_momentum, up_momentum,
        down_momentum,
    )
    grads = (query_grad, key_grad, value_grad, output_grad, gate_grad, up_grad, down_grad)
    velocities = [DECAY * momentum + grad for momentum, grad in zip(momenta, grads)]
    low = [velocity.astype(BF16) for velocity in velocities]

    def fold_down(block):
        turned = block.T
        return jnp.concatenate([turned[:, p * CF : (p + 1) * CF] for p in range(ratio)], axis=0)

    def unfold_down(block):
        return jnp.concatenate([block[p * CD : (p + 1) * CD] for p in range(ratio)], axis=1).T

    third = CF - R
    kv_turned = jnp.concatenate([low[1].T, low[2].T], axis=0)
    mixed_block = jnp.concatenate(
        [
            jnp.concatenate([low[0].T, low[3].T], axis=0),
            jnp.concatenate([kv_turned[:, i : i + third] for i in range(0, R, third)], axis=0),
        ],
        axis=1,
    )
    groups = jnp.stack([low[4], fold_down(low[6]), low[5], mixed_block])
    current = groups.reshape(2, 2, 1, R, CF)
    for step, mask in enumerate(fmasks):
        if step < 2:
            bit = jnp.where((fi & mask) != 0, 1, 0)
            keep = lax.dynamic_index_in_dim(current, bit, 0, keepdims=False)
            send = lax.dynamic_index_in_dim(current, 1 - bit, 0, keepdims=False)
        else:
            keep = send = current
        other = swap(send, "fsdp", F, mask)
        current = jnp.concatenate([keep, other], axis=-3)
    block = current
    owner_f = [g * (F // 4) for g in range(4)]
    owner_k = [2, 5, 2, 5] if C == 8 else [(5 * g + 2) % C for g in range(4)]
    gathered = [block]
    for r in range(1, C):
        pairs = [((owner_k[g] ^ r) * F + owner_f[g], owner_k[g] * F + owner_f[g]) for g in range(4)]
        gathered.append(lax.ppermute(block, ("ctx", "fsdp"), pairs))

    owner = jnp.zeros((), jnp.bool_)
    for g in range(4):
        owner = owner | ((fi == owner_f[g]) & (kc == owner_k[g]))
    kind = jnp.where(fi == owner_f[3], 3, jnp.where(fi == owner_f[1], 2, 1))
    role = jnp.where(owner, kind, 0).astype(jnp.int32).reshape(1)
    replies = owner_step(role, gathered, F, C)
    reply = jnp.where(owner, replies[0], jnp.zeros_like(replies[0]))
    for r in range(1, C):
        pairs = [(owner_k[g] * F + owner_f[g], (owner_k[g] ^ r) * F + owner_f[g]) for g in range(4)]
        reply = reply + lax.ppermute(replies[r], ("ctx", "fsdp"), pairs)
    current = reply
    for step in reversed(range(len(fmasks))):
        mask = fmasks[step]
        size = current.shape[-3] // 2
        keep = lax.slice_in_dim(current, 0, size, axis=current.ndim - 3)
        send = lax.slice_in_dim(current, size, 2 * size, axis=current.ndim - 3)
        other = swap(send, "fsdp", F, mask)
        high = (fi & mask) != 0
        if step < 2:
            current = jnp.stack([jnp.where(high, other, keep), jnp.where(high, keep, other)])
        else:
            current = jnp.where(high, other, keep)
    ortho_groups = current.reshape(4, R, CF)
    mixed = ortho_groups[3]
    kv_ortho = jnp.concatenate(
        [mixed[i : i + 2 * CK, R:] for i in range(0, R, 2 * CK)], axis=1
    )
    orthos = [
        mixed[:CD, :R].T,
        kv_ortho[:CK].T,
        kv_ortho[CK:].T,
        mixed[CD:, :R].T,
        ortho_groups[0],
        ortho_groups[2],
        unfold_down(ortho_groups[1]),
    ]
    weights = (
        query_weight, key_weight, value_weight, output_weight, gate_weight, up_weight, down_weight,
    )
    fans = (D, D, D, 1, D, D, FF)
    shapes = ((D, QW), (D, KW), (D, KW), (QW, D), (D, FF), (D, FF), (FF, D))
    updated = []
    for number in range(7):
        total = shapes[number][1]
        width = total // C
        chosen = (
            lax.broadcasted_iota(jnp.int32, (total, width), 0)
            == lax.broadcasted_iota(jnp.int32, (total, width), 1) + kc * width
        ).astype(BF16)
        step_size = STEP_RATE * math.sqrt(max(shapes[number]) / fans[number])
        own = einsum("rc,cw->rw", weights[number], chosen)
        updated.append(own - step_size * orthos[number].astype(F32))
    gain_rate = STEP_RATE / math.sqrt(S * F * L * C)
    first_velocity = DECAY * first_momentum + first_grad
    second_velocity = DECAY * second_momentum + second_grad
    first_updated = first_gain.astype(F32) - gain_rate * first_velocity
    second_updated = second_gain.astype(F32) - gain_rate * second_velocity
    return (
        (layer_output.reshape(S, L, D), input_grad.reshape(S, L, D))
        + grads
        + (first_grad, second_grad)
        + tuple(updated)
        + (first_updated, second_updated)
        + tuple(velocities)
        + (first_velocity, second_velocity)
    )


def solution(mesh):
    rows = P("fsdp", None)
    block = P("fsdp", "ctx")
    line = P("fsdp")
    stream = P("fsdp", "ctx", None)
    in_specs = (stream, stream, block) + (rows,) * 7 + (line,) * 2 + (block,) * 7 + (line,) * 2
    out_specs = (stream, stream) + ((block,) * 7 + (line,) * 2) * 3
    return jax.shard_map(local, mesh=mesh, in_specs=in_specs, out_specs=out_specs, check_vma=False)
```
